32 devices in a mesh: lat: 16 (over z, y, x), ray: 2 (over core).
Axes of the slice: x: 2, y: 2, z: 4, core: 2. Of those that a mesh axis runs over, the one named last changes fastest.
Arguments:
- kernels: float32 [256, 4, 128, 128], P(('lat', 'ray')), may hold values from -0.25 to 0.25
- pattern: int32 [256, 4], P(('lat', 'ray')), may hold values from 0 to 255, as said below
- offsets: int32 [4], replicated, may hold values from 1 to 128, as said below
- smooth_weight: float32 [4, 256, 128], P(None, 'lat'), may hold values from 0.2 to 1
- u_data: float32 [256, 128], P(('lat', 'ray')), may hold values from -16 to 16
- u_smooth: float32 [4, 256, 128], P(None, 'lat'), may hold values from -6 to 6
- right_vector: float32 [256, 128], P('lat'), may hold values from -16 to 16
- direction: float32 [256, 128], P('lat'), may hold values from -6 to 6
- model_estimate: float32 [256, 128], P('lat'), may hold values from -6 to 6
- recurrence: float32 [3], replicated, may hold values from 0.5 to 2
Outputs:
- u_data_new: float32 [256, 128], P(('lat', 'ray'))
- u_smooth_new: float32 [4, 256, 128], P(None, 'lat')
- v_new: float32 [256, 128], P('lat')
- w_new: float32 [256, 128], P('lat')
- x_new: float32 [256, 128], P('lat')
- scalars: float32 [4], replicated
The draws below stay inside these ranges and needn't reach their ends.
Inputs may be any that keep to these rules, and one draw needn't show every extreme that they name: `pattern`: in each aligned block of 8 ray blocks (the rows of one device), the tiles of any one longitude band are named by exactly 2 kernel blocks or by none; kernel blocks of the same rows that name the same band name different tiles; the 4 tiles of a ray block differ. `offsets`: the last offset is 128.
All inputs are finite; a program needn't handle non-finite values.
Results may differ from the reference program's by a relative error of at most 0.00007.
Values sent between devices are 32-bit elements; how exact they have to be, the bound alone decides.
A program may use at most 64 MiB of HBM per device.

```python
import math
import jax
import jax.numpy as jnp
from jax import lax

BLOCK = 128
K = 4
S = 4
RB_DEV = 8
TILE_DEV = 16
NRB = 256
NT = 256
NCELL = 32768
ROWS_ALL = 163840
CAP = 2


def scaled_field(key, rows, cols):
    key_base, key_rows, key_cols = jax.random.split(key, 3)
    base = jnp.clip(jax.random.normal(key_base, (rows, cols), jnp.float32), -4.0, 4.0)
    row_f = jnp.exp(jax.random.uniform(key_rows, (rows, 1), jnp.float32, 0.0, math.log(3.3)))
    col_f = jnp.exp(jax.random.uniform(key_cols, (1, cols), jnp.float32, 0.0, math.log(3.3)))
    ramp = 1.0 + 2.0 * jnp.arange(rows, dtype=jnp.float32)[:, None] / max(rows - 1, 1)
    return 0.115 * base * row_f * col_f * ramp


def draw_u_data(key, part):
    return scaled_field(jax.random.fold_in(key, 11), NRB, BLOCK)


def draw_right_vector(key, part):
    return scaled_field(jax.random.fold_in(key, 23), NT, BLOCK)


def draw_offsets(key, part):
    base = jax.random.randint(jax.random.fold_in(key, 37), (S,), 1, BLOCK + 1)
    return base.at[S - 1].set(BLOCK).astype(jnp.int32)


def draw_pattern(key, part):
    device_total = NRB // RB_DEV
    band_total = NT // TILE_DEV
    slot_total = RB_DEV * K
    group_total = (slot_total + CAP - 1) // CAP
    device_keys = jax.random.split(jax.random.fold_in(key, 41), device_total)
    band_order = jax.vmap(lambda one_key: jax.random.permutation(one_key, band_total))(device_keys)[:, :group_total]
    start_tiles = jax.random.randint(jax.random.fold_in(key, 43), (device_total, group_total), 0, TILE_DEV)
    slot_ids = jnp.arange(slot_total, dtype=jnp.int32)
    group_of = slot_ids // CAP
    rank_of = slot_ids % CAP
    tile_ids = band_order[:, group_of] * TILE_DEV + (start_tiles[:, group_of] + rank_of[None, :]) % TILE_DEV
    shuffle_keys = jax.random.split(jax.random.fold_in(key, 47), device_total)
    shuffled = jax.vmap(lambda one_key, row_ids: jax.random.permutation(one_key, row_ids))(shuffle_keys, tile_ids)
    return shuffled.reshape(NRB, K).astype(jnp.int32)


def block_levels(stream_key, extent, cuts, smallest, top_value):
    factor_of = 1.0
    for axis_at, shards_of in cuts:
        draws = jax.random.uniform(jax.random.fold_in(jax.random.fold_in(stream_key, 6), axis_at), (shards_of,), jnp.float32, smallest / len(cuts), top_value / len(cuts))
        factor_of = factor_of * jnp.repeat(jnp.exp(draws), extent[axis_at] // shards_of).reshape((-1,) + (1,) * (len(extent) - 1 - axis_at))
    return factor_of


def gaussian(stream_key, dims, width, limit, cuts=(), kind=jnp.bfloat16):
    result = width * jax.random.normal(stream_key, dims, jnp.float32)
    if cuts:
        result = result * block_levels(stream_key, dims, cuts, -0.22, 0.18)
    return jnp.clip(result, -limit, limit).astype(kind)


def setup_inputs(seed: int = 0) -> dict:
    seeds = jax.random.split(jax.random.key(seed), 11)
    kernels = gaussian(seeds[0], (NRB, K, BLOCK, BLOCK), (K * BLOCK) ** -0.5, 0.25, ((0, 32),), jnp.float32)
    pattern = draw_pattern(jax.random.fold_in(seeds[10], 71), 0)
    offsets = draw_offsets(jax.random.fold_in(seeds[10], 71), 0)
    smooth_weight = jnp.clip(jnp.exp(math.log(1.0) - 1.609438 * jax.random.uniform(seeds[3], (S, NT, BLOCK), jnp.float32) ** block_levels(seeds[3], (S, NT, BLOCK), ((1, 16),), -0.2, 0.2)), 0.2, 1.0)
    u_data = draw_u_data(jax.random.fold_in(seeds[10], 71), 0)
    u_smooth = gaussian(seeds[5], (S, NT, BLOCK), 1.0, 6.0, ((1, 16),), jnp.float32)
    right_vector = draw_right_vector(jax.random.fold_in(seeds[10], 71), 0)
    direction = gaussian(seeds[7], (NT, BLOCK), 1.0, 6.0, ((0, 16),), jnp.float32)
    model_estimate = gaussian(seeds[8], (NT, BLOCK), 1.0, 6.0, ((0, 16),), jnp.float32)
    recurrence = jnp.clip(jax.random.uniform(seeds[9], (3,), jnp.float32, 0.5, 2.0), 0.5, 2.0)
    return dict(kernels=kernels, pattern=pattern, offsets=offsets, smooth_weight=smooth_weight, u_data=u_data, u_smooth=u_smooth, right_vector=right_vector, direction=direction, model_estimate=model_estimate, recurrence=recurrence)


def reference(kernels, pattern, offsets, smooth_weight, u_data, u_smooth, right_vector, direction, model_estimate, recurrence):
    highest = lax.Precision.HIGHEST
    eps = 1e-06
    alpha_old = recurrence[0]
    rhobar_old = recurrence[1]
    phibar_old = recurrence[2]
    picked = right_vector[pattern]
    data_raw = jnp.einsum('bkij,bkj->bi', kernels, picked, precision=highest) - alpha_old * u_data
    flat = right_vector.reshape(-1)
    extended = jnp.concatenate([flat, flat[:BLOCK]])
    ahead = jnp.stack([lax.dynamic_slice_in_dim(extended, offsets[s].astype(jnp.int32), NCELL) for s in range(S)])
    smooth_raw = smooth_weight * (flat[None, :] - ahead).reshape(S, NT, BLOCK) - alpha_old * u_smooth
    row_sq = jnp.sum(data_raw * data_raw) + jnp.sum(smooth_raw * smooth_raw)
    beta = jnp.sqrt(row_sq / ROWS_ALL + eps)
    terms = jnp.einsum('bkij,bi->bkj', kernels, data_raw, precision=highest)
    adjoint = jnp.zeros((NT, BLOCK), jnp.float32).at[pattern].add(terms)
    weighted = (smooth_weight * smooth_raw).reshape(S, NCELL)
    padded = jnp.concatenate([weighted[:, NCELL - BLOCK:], weighted], axis=1)
    behind = jnp.stack([lax.dynamic_slice_in_dim(padded[s], (BLOCK - offsets[s]).astype(jnp.int32), NCELL) for s in range(S)])
    adjoint = adjoint + lax.optimization_barrier(jnp.sum(weighted - behind, axis=0)).reshape(NT, BLOCK)
    ratio = NCELL / ROWS_ALL
    v_raw = ratio * adjoint / beta - beta * right_vector
    alpha = jnp.sqrt(jnp.sum(v_raw * v_raw) / NCELL + eps)
    v_new = v_raw / alpha
    rho = jnp.sqrt(rhobar_old * rhobar_old + beta * beta)
    cosine = rhobar_old / rho
    sine = beta / rho
    theta = sine * alpha
    rhobar = -cosine * alpha
    phi = cosine * phibar_old
    phibar = sine * phibar_old
    x_new = model_estimate + phi / rho * direction
    w_new = v_new - theta / rho * direction
    scalars = jnp.stack([alpha, beta, rhobar, phibar])
    return (data_raw / beta, smooth_raw / beta, v_new, w_new, x_new, scalars)
```

```python
import functools

import jax
import jax.numpy as jnp
from jax import lax
from jax.experimental import pallas as pl
from jax.experimental.pallas import tpu as pltpu
from jax.sharding import PartitionSpec as P

EPS = 1e-06
MESH = pl.DeviceIdType.MESH
F32 = jnp.float32
HIGHEST = lax.Precision.HIGHEST
ROWS = 4
GROUP = 32


def kernel(
    n_lat,
    n_ray,
    pattern,
    offsets,
    recurrence,
    kernels_hbm,
    smooth_weight,
    u_data,
    u_smooth,
    right_vector,
    direction,
    model_estimate,
    u_data_new,
    u_smooth_new,
    v_new,
    w_new,
    x_new,
    scalars,
    held,
    full,
    window,
    padded,
    smooth_raw,
    data_raw,
    contrib,
    message,
    inbox,
    square,
    squares,
    local_sem,
    send_sem,
    recv_sem,
):
    lat = lax.axis_index("lat")
    ray = lax.axis_index("ray")
    n_dev = n_lat * n_ray
    me = lat * n_ray + ray
    blocks_dev, kernel_count, block, _ = held.shape
    tiles_dev = right_vector.shape[0]
    stencil = smooth_weight.shape[0]
    slots = blocks_dev * kernel_count
    cell_count = n_lat * tiles_dev * block
    rows_all = n_dev * blocks_dev * block + stencil * cell_count
    ratio = cell_count / rows_all

    fetch = pltpu.make_async_copy(kernels_hbm, held, local_sem.at[0])
    fetch.start()
    own_band = pltpu.make_async_copy(
        right_vector, full.at[pl.ds(lat * tiles_dev, tiles_dev)], local_sem.at[1]
    )
    own_band.start()

    barrier = pltpu.get_barrier_semaphore()

    def greet(step, carry):
        other = lax.rem(me + step, n_dev)
        pl.semaphore_signal(
            barrier,
            inc=1,
            device_id=(lax.div(other, n_ray), lax.rem(other, n_ray)),
            device_id_type=MESH,
        )
        return carry

    lax.fori_loop(1, n_dev, greet, 0)
    pl.semaphore_wait(barrier, n_dev - 1)

    def send_band(step, carry):
        pltpu.make_async_remote_copy(
            src_ref=right_vector,
            dst_ref=full.at[pl.ds(lat * tiles_dev, tiles_dev)],
            send_sem=send_sem.at[0],
            recv_sem=recv_sem.at[0],
            device_id=(lax.rem(lat + step, n_lat), ray),
            device_id_type=MESH,
        ).start()
        return carry

    lax.fori_loop(1, n_lat, send_band, 0)

    alpha_old = recurrence[0]
    lane_slot = lax.broadcasted_iota(jnp.int32, (1, slots), 1)
    tile_row = jnp.zeros((1, slots), F32)
    for b in range(blocks_dev):
        for k in range(kernel_count):
            tile_row = jnp.where(
                lane_slot == b * kernel_count + k, pattern[b, k].astype(F32), tile_row
            )
    shape = (n_lat * ROWS, slots)
    message_row = lax.broadcasted_iota(jnp.int32, shape, 0)
    slot = lax.broadcasted_iota(jnp.int32, shape, 1).astype(F32)
    kind = message_row & (ROWS - 1)
    local_tile = tile_row - ((message_row // ROWS) * tiles_dev).astype(F32)
    in_band = (local_tile >= 0) & (local_tile < tiles_dev)
    first = jnp.min(jnp.where(in_band, slot, F32(slots)), axis=1, keepdims=True)
    is_first = in_band & (slot == first)
    is_second = in_band & (slot != first)
    selector = jnp.where(
        (is_first & (kind == 0)) | (is_second & (kind == 1)), F32(1), F32(0)
    )
    first_tile = jnp.sum(jnp.where(is_first, local_tile + 1, F32(0)), axis=1, keepdims=True)
    second_tile = jnp.sum(jnp.where(is_second, local_tile + 1, F32(0)), axis=1, keepdims=True)
    wide = (n_lat * ROWS, block)
    lane_wide = lax.broadcasted_iota(jnp.int32, wide, 1)
    kind_wide = lax.broadcasted_iota(jnp.int32, wide, 0) & (ROWS - 1)
    mark = lax.rem(me, GROUP) * ROWS
    header = jnp.where(
        lane_wide == mark,
        first_tile,
        jnp.where(lane_wide == mark + 1, second_tile, F32(0)),
    )
    header = jnp.where(kind_wide == 2, header, F32(0))
    is_total = (kind_wide == 2) & (lane_wide == mark + 2)

    fetch.wait()
    own_band.wait()
    rest = pl.ds(0, (n_lat - 1) * tiles_dev)
    bands = pltpu.make_async_remote_copy(
        src_ref=full.at[rest],
        dst_ref=full.at[rest],
        send_sem=send_sem.at[0],
        recv_sem=recv_sem.at[0],
        device_id=(lat, ray),
        device_id_type=MESH,
    )
    bands.wait_recv()

    diagonal = lax.broadcasted_iota(jnp.int32, (block, block), 0) == lax.broadcasted_iota(
        jnp.int32, (block, block), 1
    )
    for b in range(blocks_dev):
        total = jnp.where(diagonal, -alpha_old * u_data[b : b + 1, :], F32(0))
        for k in range(kernel_count):
            total = total + held[b, k] * full[pl.ds(pattern[b, k], 1), :]
        column = jnp.sum(total, axis=1, keepdims=True)
        data_raw[b : b + 1, :] = jnp.sum(
            jnp.where(diagonal, column, F32(0)), axis=0, keepdims=True
        )
        for k in range(kernel_count):
            contrib[b * kernel_count + k : b * kernel_count + k + 1, :] = jnp.sum(
                held[b, k] * column, axis=0, keepdims=True
            )

    own = right_vector[...]
    lane = lax.broadcasted_iota(jnp.int32, (1, block), 1)
    window[0:tiles_dev, :] = own
    window[tiles_dev : tiles_dev + 1, :] = full[
        pl.ds(lax.rem(lat + 1, n_lat) * tiles_dev, 1), :
    ]
    below = window[1 : tiles_dev + 1, :]
    rim = jnp.zeros((1, block), F32)
    smooth_square = jnp.zeros((tiles_dev, block), F32)
    for s in range(stencil):
        offset = offsets[s]
        back = (block - offset) & (block - 1)
        ahead = jnp.where(
            lane < block - offset, pltpu.roll(own, back, 1), pltpu.roll(below, back, 1)
        )
        raw = smooth_weight[s] * (own - ahead) - alpha_old * u_smooth[s]
        smooth_raw[s] = raw
        smooth_square = smooth_square + raw * raw
        weighted = smooth_weight[s] * raw
        padded[s, 8 : 8 + tiles_dev, :] = weighted
        turned = pltpu.roll(weighted, offset & (block - 1), 1)
        rim = rim + jnp.where(lane < offset, turned[tiles_dev - 1 : tiles_dev, :], F32(0))
    raw = data_raw[...]
    row_sum = jnp.sum(raw * raw, axis=0, keepdims=True) + (
        jnp.sum(smooth_square, axis=0, keepdims=True) * (1.0 / n_ray)
    )
    local_total = jnp.sum(row_sum, axis=1, keepdims=True)

    picked = jnp.dot(selector, contrib[...], precision=HIGHEST, preferred_element_type=F32)
    outgoing = (
        picked
        + header
        + jnp.where(is_total, local_total, F32(0))
        + jnp.where(kind_wide == 3, rim, F32(0))
    )
    for band in range(n_lat):
        message[band] = outgoing[band * ROWS : (band + 1) * ROWS, :]

    def send_message(step, carry):
        other = lax.rem(me + step, n_dev)
        pltpu.make_async_remote_copy(
            src_ref=message.at[lax.div(other, n_ray)],
            dst_ref=inbox.at[me],
            send_sem=send_sem.at[1],
            recv_sem=recv_sem.at[1],
            device_id=(lax.div(other, n_ray), lax.rem(other, n_ray)),
            device_id_type=MESH,
        ).start()
        return carry

    lax.fori_loop(1, n_dev, send_message, 0)
    inbox[me] = message[lat]

    smooth_adjoint = jnp.zeros((tiles_dev, block), F32)
    for s in range(stencil):
        offset = offsets[s]
        padded[s, 7:8, :] = jnp.zeros((1, block), F32)
        weighted = padded[s, 8 : 8 + tiles_dev, :]
        above = padded[s, 7 : 7 + tiles_dev, :]
        behind = jnp.where(
            lane >= offset,
            pltpu.roll(weighted, offset & (block - 1), 1),
            pltpu.roll(above, offset & (block - 1), 1),
        )
        smooth_adjoint = smooth_adjoint + (weighted - behind)

    bands.wait_send()
    others = pl.ds(0, n_dev - 1)
    messages = pltpu.make_async_remote_copy(
        src_ref=inbox.at[others],
        dst_ref=inbox.at[others],
        send_sem=send_sem.at[1],
        recv_sem=recv_sem.at[1],
        device_id=(lat, ray),
        device_id_type=MESH,
    )
    messages.wait_recv()

    group = min(GROUP, n_dev)
    lane_group = lax.broadcasted_iota(jnp.int32, (1, group * ROWS), 1)
    tile_group = lax.broadcasted_iota(jnp.int32, (tiles_dev, group * ROWS), 0)
    lane_kind = lane_group & (ROWS - 1)
    west = lax.rem(lat + n_lat - 1, n_lat) * n_ray
    adjoint = smooth_adjoint
    row_total = jnp.zeros((1, 1), F32)
    for start in range(0, n_dev, group):
        letters = inbox[start : start + group]
        heads = jnp.sum(letters[:, 2, :], axis=0, keepdims=True)[:, : group * ROWS]
        row_total = row_total + jnp.sum(
            jnp.where(lane_kind == 2, heads, F32(0)), axis=1, keepdims=True
        )
        place = jnp.where(
            (lane_kind < 2) & (heads == (tile_group + 1).astype(F32)), F32(1), F32(0)
        )
        place = jnp.where(
            (tile_group == 0) & (lane_group == (west - start) * ROWS + 3), F32(-1), place
        )
        adjoint = adjoint + jnp.dot(
            place,
            letters.reshape(group * ROWS, block),
            precision=HIGHEST,
            preferred_element_type=F32,
        )

    beta = jnp.sqrt(row_total / rows_all + EPS)
    v_raw = ratio * adjoint / beta - beta * own
    square_row = jnp.sum(v_raw * v_raw, axis=0, keepdims=True)
    square[...] = square_row
    squares[lat] = square_row

    def send_square(step, carry):
        pltpu.make_async_remote_copy(
            src_ref=square,
            dst_ref=squares.at[lat],
            send_sem=send_sem.at[2],
            recv_sem=recv_sem.at[2],
            device_id=(lax.rem(lat + step, n_lat), ray),
            device_id_type=MESH,
        ).start()
        return carry

    lax.fori_loop(1, n_lat, send_square, 0)

    rhobar_old = recurrence[1]
    phibar_old = recurrence[2]
    rho = jnp.sqrt(rhobar_old * rhobar_old + beta * beta)
    cosine = rhobar_old / rho
    sine = beta / rho
    phi = cosine * phibar_old
    phibar = sine * phibar_old
    u_data_new[...] = data_raw[...] / beta
    for s in range(stencil):
        u_smooth_new[s] = smooth_raw[s] / beta
    x_new[...] = model_estimate[...] + phi / rho * direction[...]
    messages.wait_send()

    peers = pl.ds(0, n_lat - 1)
    sums = pltpu.make_async_remote_copy(
        src_ref=squares.at[peers],
        dst_ref=squares.at[peers],
        send_sem=send_sem.at[2],
        recv_sem=recv_sem.at[2],
        device_id=(lat, ray),
        device_id_type=MESH,
    )
    sums.wait_recv()
    model_square = jnp.sum(jnp.sum(squares[...], axis=0), axis=1, keepdims=True)
    alpha = jnp.sqrt(model_square / cell_count + EPS)
    theta = sine * alpha
    new = v_raw / alpha
    v_new[...] = new
    w_new[...] = new - theta / rho * direction[...]
    scalars[0] = alpha[0, 0]
    scalars[1] = beta[0, 0]
    scalars[2] = (-cosine * alpha)[0, 0]
    scalars[3] = phibar[0, 0]
    sums.wait_send()


def local(
    kernels,
    pattern,
    offsets,
    smooth_weight,
    u_data,
    u_smooth,
    right_vector,
    direction,
    model_estimate,
    recurrence,
):
    n_lat = lax.axis_size("lat")
    n_ray = lax.axis_size("ray")
    n_dev = n_lat * n_ray
    blocks_dev, kernel_count, block, _ = kernels.shape
    tiles_dev = right_vector.shape[0]
    stencil = offsets.shape[0]
    smem = pl.BlockSpec(memory_space=pltpu.SMEM)
    vmem = pl.BlockSpec(memory_space=pltpu.VMEM)
    like = lambda x: jax.ShapeDtypeStruct(x.shape, F32)
    return pl.pallas_call(
        functools.partial(kernel, n_lat, n_ray),
        out_shape=(
            like(u_data),
            like(u_smooth),
            like(right_vector),
            like(right_vector),
            like(right_vector),
            jax.ShapeDtypeStruct((4,), F32),
        ),
        in_specs=[smem] * 3 + [pl.BlockSpec(memory_space=pl.ANY)] + [vmem] * 6,
        out_specs=(vmem, vmem, vmem, vmem, vmem, smem),
        scratch_shapes=[
            pltpu.VMEM(kernels.shape, F32),
            pltpu.VMEM((n_lat * tiles_dev, block), F32),
            pltpu.VMEM((tiles_dev + 8, block), F32),
            pltpu.VMEM((stencil, tiles_dev + 8, block), F32),
            pltpu.VMEM((stencil, tiles_dev, block), F32),
            pltpu.VMEM((blocks_dev, block), F32),
            pltpu.VMEM((blocks_dev * kernel_count, block), F32),
            pltpu.VMEM((n_lat, ROWS, block), F32),
            pltpu.VMEM((n_dev, ROWS, block), F32),
            pltpu.VMEM((1, block), F32),
            pltpu.VMEM((n_lat, 1, block), F32),
            pltpu.SemaphoreType.DMA((2,)),
            pltpu.SemaphoreType.DMA((3,)),
            pltpu.SemaphoreType.DMA((3,)),
        ],
        compiler_params=pltpu.CompilerParams(collective_id=0, has_side_effects=True),
    )(
        pattern,
        offsets,
        recurrence,
        kernels,
        smooth_weight,
        u_data,
        u_smooth,
        right_vector,
        direction,
        model_estimate,
    )


def solution(mesh):
    return jax.shard_map(
        local,
        mesh=mesh,
        in_specs=(
            P(("lat", "ray"), None, None, None),
            P(("lat", "ray"), None),
            P(),
            P(None, "lat", None),
            P(("lat", "ray"), None),
            P(None, "lat", None),
            P("lat", None),
            P("lat", None),
            P("lat", None),
            P(),
        ),
        out_specs=(
            P(("lat", "ray"), None),
            P(None, "lat", None),
            P("lat", None),
            P("lat", None),
            P("lat", None),
            P(),
        ),
        check_vma=False,
    )
```

```python
import functools

import jax
import jax.numpy as jnp
from jax import lax
from jax.experimental import pallas as pl
from jax.experimental.pallas import tpu as pltpu
from jax.sharding import PartitionSpec as P

EPS = 1e-06
MESH = pl.DeviceIdType.MESH
F32 = jnp.float32
HIGHEST = lax.Precision.HIGHEST
ROWS = 4
VMEM_BYTES = 16 * 1024 * 1024
GROUP = 32


def plane_size(n_lat):
    return 4 if n_lat % 4 == 0 else 1


def partner(at, step, count):
    if count & (count - 1):
        return lax.rem(at + step, count)
    result, bit = 0, 1
    while bit < count:
        result = result + bit * lax.rem(lax.div(at, bit) + step // bit, 2)
        bit *= 2
    return result


def source(at, step, count):
    return partner(at, count - step if count & (count - 1) else step, count)


def each(count, body):
    if count <= 64:
        for step in range(count - 1, 0, -1):
            body(step)
    else:
        lax.fori_loop(1, count, lambda step, carry: (body(count - step), carry)[1], 0)


def deliver(*refs):
    half = (len(refs) - 1) // 2
    sems = refs[-1]
    copies = [
        pltpu.make_async_copy(refs[at], refs[half + at], sems.at[at]) for at in range(half)
    ]
    for copy in copies:
        copy.start()
    for copy in copies:
        copy.wait()


def kernel(
    n_lat,
    n_ray,
    pattern_in,
    offsets_in,
    recurrence_in,
    kernels_in,
    smooth_weight_in,
    u_data_in,
    u_smooth_in,
    right_vector_in,
    direction_in,
    model_estimate_in,
    u_data_new,
    u_smooth_new,
    v_new,
    w_new,
    x_new,
    scalars,
    pattern,
    offsets,
    recurrence,
    held,
    smooth_weight,
    u_data,
    u_smooth,
    direction,
    model_estimate,
    full,
    window,
    padded,
    smooth_raw,
    data_raw,
    contrib,
    message,
    inbox,
    square,
    squares,
    local_sem,
    band_sem,
    send_sem,
    recv_sem,
):
    lat = lax.axis_index("lat")
    ray = lax.axis_index("ray")
    n_dev = n_lat * n_ray
    me = lat * n_ray + ray
    blocks_dev, kernel_count, block, _ = held.shape
    tiles_dev = right_vector_in.shape[0]
    stencil = smooth_weight.shape[0]
    slots = blocks_dev * kernel_count
    cell_count = n_lat * tiles_dev * block
    rows_all = n_dev * blocks_dev * block + stencil * cell_count
    ratio = cell_count / rows_all

    n_inner = plane_size(n_lat)
    n_outer = n_lat // n_inner
    outer, inner = lax.div(lat, n_inner), lax.rem(lat, n_inner)

    barrier = pltpu.get_barrier_semaphore()

    def greet(device):
        pl.semaphore_signal(barrier, inc=1, device_id=device, device_id_type=MESH)

    for step in range(n_outer - 1, 0, -1):
        greet((partner(outer, step, n_outer) * n_inner + inner, ray))
    for step in range(1, n_inner):
        greet((outer * n_inner + partner(inner, step, n_inner), ray))
    for step in range(1, n_ray):
        greet((lat, partner(ray, step, n_ray)))

    def band_of(index):
        return full.at[pl.ds(pl.multiple_of(index * tiles_dev, tiles_dev), tiles_dev)]

    own_band = pltpu.make_async_copy(right_vector_in, band_of(lat), local_sem.at[0])
    own_band.start()
    fetches = [
        pltpu.make_async_copy(source, target, local_sem.at[1 + at])
        for at, (source, target) in enumerate(
            (
                (pattern_in, pattern),
                (offsets_in, offsets),
                (recurrence_in, recurrence),
                (smooth_weight_in, smooth_weight),
                (u_data_in, u_data),
                (u_smooth_in, u_smooth),
                (direction_in, direction),
                (model_estimate_in, model_estimate),
                (kernels_in, held),
            )
        )
    ]
    for fetch in fetches:
        fetch.start()
    own_band.wait()
    pl.semaphore_wait(barrier, n_outer + n_inner + n_ray - 3)

    def copy_band(index, slot, device):
        return pltpu.make_async_remote_copy(
            src_ref=band_of(index),
            dst_ref=band_of(index),
            send_sem=send_sem.at[0],
            recv_sem=band_sem.at[slot],
            device_id=device,
            device_id_type=MESH,
        )

    def forward(index, slot):
        for step in range(n_inner - 1, 0, -1):
            copy_band(
                index, slot * n_inner + step, (outer * n_inner + partner(inner, step, n_inner), ray)
            ).start()

    for step in range(n_outer - 1, 0, -1):
        copy_band(
            lat, step * n_inner, (partner(outer, step, n_outer) * n_inner + inner, ray)
        ).start()
    forward(lat, 0)
    for fetch in fetches[:3]:
        fetch.wait()

    alpha_old = recurrence[0]
    lane_slot = lax.broadcasted_iota(jnp.int32, (1, slots), 1)
    tile_row = jnp.zeros((1, slots), F32)
    for b in range(blocks_dev):
        for k in range(kernel_count):
            tile_row = jnp.where(
                lane_slot == b * kernel_count + k, pattern[k, b].astype(F32), tile_row
            )
    shape = (n_lat * ROWS, slots)
    message_row = lax.broadcasted_iota(jnp.int32, shape, 0)
    slot = lax.broadcasted_iota(jnp.int32, shape, 1).astype(F32)
    kind = message_row & (ROWS - 1)
    local_tile = tile_row - ((message_row // ROWS) * tiles_dev).astype(F32)
    in_band = (local_tile >= 0) & (local_tile < tiles_dev)
    first = jnp.min(jnp.where(in_band, slot, F32(slots)), axis=1, keepdims=True)
    is_first = in_band & (slot == first)
    is_second = in_band & (slot != first)
    selector = jnp.where(
        (is_first & (kind == 0)) | (is_second & (kind == 1)), F32(1), F32(0)
    )
    first_tile = jnp.sum(jnp.where(is_first, local_tile + 1, F32(0)), axis=1, keepdims=True)
    second_tile = jnp.sum(jnp.where(is_second, local_tile + 1, F32(0)), axis=1, keepdims=True)
    wide = (n_lat * ROWS, block)
    lane_wide = lax.broadcasted_iota(jnp.int32, wide, 1)
    kind_wide = lax.broadcasted_iota(jnp.int32, wide, 0) & (ROWS - 1)
    mark = lax.rem(me, GROUP) * ROWS
    header = jnp.where(
        lane_wide == mark,
        first_tile,
        jnp.where(lane_wide == mark + 1, second_tile, F32(0)),
    )
    header = jnp.where(kind_wide == 2, header, F32(0))
    is_total = (kind_wide == 2) & (lane_wide == mark + 2)

    for step in range(1, n_outer):
        index = source(outer, step, n_outer) * n_inner + inner
        copy_band(index, step * n_inner, (lat, ray)).wait_recv()
        forward(index, step)
    for fetch in fetches[3:]:
        fetch.wait()
    for step in range(n_outer):
        column = source(outer, step, n_outer) * n_inner
        for turn in range(1, n_inner):
            copy_band(
                column + source(inner, turn, n_inner), step * n_inner + turn, (lat, ray)
            ).wait_recv()

    diagonal = lax.broadcasted_iota(jnp.int32, (block, block), 0) == lax.broadcasted_iota(
        jnp.int32, (block, block), 1
    )
    for b in range(blocks_dev):
        total = jnp.where(diagonal, -alpha_old * u_data[b : b + 1, :], F32(0))
        for k in range(kernel_count):
            total = total + held[b, k] * full[pl.ds(pattern[k, b], 1), :]
        column = jnp.sum(total, axis=1, keepdims=True)
        data_raw[b : b + 1, :] = jnp.sum(
            jnp.where(diagonal, column, F32(0)), axis=0, keepdims=True
        )
        for k in range(kernel_count):
            contrib[b * kernel_count + k : b * kernel_count + k + 1, :] = jnp.sum(
                held[b, k] * column, axis=0, keepdims=True
            )

    own = full[pl.ds(pl.multiple_of(lat * tiles_dev, tiles_dev), tiles_dev), :]
    lane = lax.broadcasted_iota(jnp.int32, (1, block), 1)
    window[0:tiles_dev, :] = own
    window[tiles_dev : tiles_dev + 1, :] = full[
        pl.ds(lax.rem(lat + 1, n_lat) * tiles_dev, 1), :
    ]
    below = window[1 : tiles_dev + 1, :]
    rim = jnp.zeros((1, block), F32)
    smooth_square = jnp.zeros((tiles_dev, block), F32)
    for s in range(stencil):
        offset = offsets[s]
        back = (block - offset) & (block - 1)
        ahead = jnp.where(
            lane < block - offset, pltpu.roll(own, back, 1), pltpu.roll(below, back, 1)
        )
        raw = smooth_weight[s] * (own - ahead) - alpha_old * u_smooth[s]
        smooth_raw[s] = raw
        smooth_square = smooth_square + raw * raw
        weighted = smooth_weight[s] * raw
        padded[s, 8 : 8 + tiles_dev, :] = weighted
        turned = pltpu.roll(weighted, offset & (block - 1), 1)
        rim = rim + jnp.where(lane < offset, turned[tiles_dev - 1 : tiles_dev, :], F32(0))
    raw = data_raw[...]
    row_sum = jnp.sum(raw * raw, axis=0, keepdims=True) + (
        jnp.sum(smooth_square, axis=0, keepdims=True) * (1.0 / n_ray)
    )
    local_total = jnp.sum(row_sum, axis=1, keepdims=True)

    picked = jnp.dot(selector, contrib[...], precision=HIGHEST, preferred_element_type=F32)
    outgoing = (
        picked
        + header
        + jnp.where(is_total, local_total, F32(0))
        + jnp.where(kind_wide == 3, rim, F32(0))
    )
    for band in range(n_lat):
        message[band] = outgoing[band * ROWS : (band + 1) * ROWS, :]

    def send_message(step):
        row = partner(lat, step // n_ray, n_lat)
        core = partner(ray, step % n_ray, n_ray)
        pltpu.make_async_remote_copy(
            src_ref=message.at[row],
            dst_ref=inbox.at[me],
            send_sem=send_sem.at[1],
            recv_sem=recv_sem.at[0],
            device_id=(row, core),
            device_id_type=MESH,
        ).start()

    each(n_dev, send_message)
    inbox[me] = message[lat]

    smooth_adjoint = jnp.zeros((tiles_dev, block), F32)
    for s in range(stencil):
        offset = offsets[s]
        padded[s, 7:8, :] = jnp.zeros((1, block), F32)
        weighted = padded[s, 8 : 8 + tiles_dev, :]
        above = padded[s, 7 : 7 + tiles_dev, :]
        behind = jnp.where(
            lane >= offset,
            pltpu.roll(weighted, offset & (block - 1), 1),
            pltpu.roll(above, offset & (block - 1), 1),
        )
        smooth_adjoint = smooth_adjoint + (weighted - behind)

    for _ in range(n_outer - 1 + n_outer * (n_inner - 1)):
        copy_band(lat, 0, (lat, ray)).wait_send()
    others = pl.ds(0, n_dev - 1)
    messages = pltpu.make_async_remote_copy(
        src_ref=inbox.at[others],
        dst_ref=inbox.at[others],
        send_sem=send_sem.at[1],
        recv_sem=recv_sem.at[0],
        device_id=(lat, ray),
        device_id_type=MESH,
    )
    messages.wait_recv()

    group = min(GROUP, n_dev)
    lane_group = lax.broadcasted_iota(jnp.int32, (1, group * ROWS), 1)
    tile_group = lax.broadcasted_iota(jnp.int32, (tiles_dev, group * ROWS), 0)
    lane_kind = lane_group & (ROWS - 1)
    west = lax.rem(lat + n_lat - 1, n_lat) * n_ray
    adjoint = smooth_adjoint
    row_total = jnp.zeros((1, 1), F32)
    for start in range(0, n_dev, group):
        letters = inbox[start : start + group]
        heads = jnp.sum(letters[:, 2, :], axis=0, keepdims=True)[:, : group * ROWS]
        row_total = row_total + jnp.sum(
            jnp.where(lane_kind == 2, heads, F32(0)), axis=1, keepdims=True
        )
        place = jnp.where(
            (lane_kind < 2) & (heads == (tile_group + 1).astype(F32)), F32(1), F32(0)
        )
        place = jnp.where(
            (tile_group == 0) & (lane_group == (west - start) * ROWS + 3), F32(-1), place
        )
        adjoint = adjoint + jnp.dot(
            place,
            letters.reshape(group * ROWS, block),
            precision=HIGHEST,
            preferred_element_type=F32,
        )

    beta = jnp.sqrt(row_total / rows_all + EPS)
    v_raw = ratio * adjoint / beta - beta * own
    square_row = jnp.sum(v_raw * v_raw, axis=0, keepdims=True)
    square[...] = square_row
    squares[lat] = square_row

    def send_square(step):
        pltpu.make_async_remote_copy(
            src_ref=square,
            dst_ref=squares.at[lat],
            send_sem=send_sem.at[2],
            recv_sem=recv_sem.at[1],
            device_id=(partner(lat, step, n_lat), ray),
            device_id_type=MESH,
        ).start()

    each(n_lat, send_square)

    rhobar_old = recurrence[1]
    phibar_old = recurrence[2]
    rho = jnp.sqrt(rhobar_old * rhobar_old + beta * beta)
    cosine = rhobar_old / rho
    sine = beta / rho
    phi = cosine * phibar_old
    phibar = sine * phibar_old
    u_data_new[...] = data_raw[...] / beta
    for s in range(stencil):
        u_smooth_new[s] = smooth_raw[s] / beta
    x_new[...] = model_estimate[...] + phi / rho * direction[...]
    messages.wait_send()

    peers = pl.ds(0, n_lat - 1)
    sums = pltpu.make_async_remote_copy(
        src_ref=squares.at[peers],
        dst_ref=squares.at[peers],
        send_sem=send_sem.at[2],
        recv_sem=recv_sem.at[1],
        device_id=(lat, ray),
        device_id_type=MESH,
    )
    sums.wait_recv()
    model_square = jnp.sum(jnp.sum(squares[...], axis=0), axis=1, keepdims=True)
    alpha = jnp.sqrt(model_square / cell_count + EPS)
    theta = sine * alpha
    new = v_raw / alpha
    v_new[...] = new
    w_new[...] = new - theta / rho * direction[...]
    scalars[0] = alpha[0, 0]
    scalars[1] = beta[0, 0]
    scalars[2] = (-cosine * alpha)[0, 0]
    scalars[3] = phibar[0, 0]
    sums.wait_send()


def local(
    kernels,
    pattern,
    offsets,
    smooth_weight,
    u_data,
    u_smooth,
    right_vector,
    direction,
    model_estimate,
    recurrence,
):
    n_lat = lax.axis_size("lat")
    n_ray = lax.axis_size("ray")
    n_dev = n_lat * n_ray
    blocks_dev, kernel_count, block, _ = kernels.shape
    tiles_dev = right_vector.shape[0]
    stencil = offsets.shape[0]
    smem = pl.BlockSpec(memory_space=pltpu.SMEM)
    vmem = pl.BlockSpec(memory_space=pltpu.VMEM)
    like = lambda x: jax.ShapeDtypeStruct(x.shape, F32)
    n_inner = plane_size(n_lat)
    results = pl.pallas_call(
        functools.partial(kernel, n_lat, n_ray),
        out_shape=(
            like(u_data),
            like(u_smooth),
            like(right_vector),
            like(right_vector),
            like(right_vector),
            jax.ShapeDtypeStruct((4,), F32),
        ),
        in_specs=[pl.BlockSpec(memory_space=pltpu.HBM)] * 10,
        out_specs=(vmem, vmem, vmem, vmem, vmem, smem),
        scratch_shapes=[
            pltpu.SMEM((kernel_count, blocks_dev), jnp.int32),
            pltpu.SMEM(offsets.shape, jnp.int32),
            pltpu.SMEM(recurrence.shape, F32),
            pltpu.VMEM(kernels.shape, F32),
            pltpu.VMEM(smooth_weight.shape, F32),
            pltpu.VMEM(u_data.shape, F32),
            pltpu.VMEM(u_smooth.shape, F32),
            pltpu.VMEM(direction.shape, F32),
            pltpu.VMEM(model_estimate.shape, F32),
            pltpu.VMEM((n_lat * tiles_dev, block), F32),
            pltpu.VMEM((tiles_dev + 8, block), F32),
            pltpu.VMEM((stencil, tiles_dev + 8, block), F32),
            pltpu.VMEM((stencil, tiles_dev, block), F32),
            pltpu.VMEM((blocks_dev, block), F32),
            pltpu.VMEM((blocks_dev * kernel_count, block), F32),
            pltpu.VMEM((n_lat, ROWS, block), F32),
            pltpu.VMEM((n_dev, ROWS, block), F32),
            pltpu.VMEM((1, block), F32),
            pltpu.VMEM((n_lat, 1, block), F32),
            pltpu.SemaphoreType.DMA((10,)),
            pltpu.SemaphoreType.DMA((n_lat,)),
            pltpu.SemaphoreType.DMA((3,)),
            pltpu.SemaphoreType.DMA((2,)),
        ],
        compiler_params=pltpu.CompilerParams(
            collective_id=0, has_side_effects=True, vmem_limit_bytes=VMEM_BYTES
        ),
    )(
        *(
            pltpu.with_memory_space_constraint(x, pltpu.HBM)
            for x in (
                pattern.T,
                offsets,
                recurrence,
                kernels,
                smooth_weight,
                u_data,
                u_smooth,
                right_vector,
                direction,
                model_estimate,
            )
        )
    )
    return pl.pallas_call(
        deliver,
        out_shape=tuple(like(x) for x in results),
        in_specs=[vmem] * 5 + [smem],
        out_specs=(pl.BlockSpec(memory_space=pltpu.HBM),) * 6,
        scratch_shapes=[pltpu.SemaphoreType.DMA((6,))],
        compiler_params=pltpu.CompilerParams(vmem_limit_bytes=VMEM_BYTES),
    )(*results)


def solution(mesh):
    return jax.shard_map(
        local,
        mesh=mesh,
        in_specs=(
            P(("lat", "ray"), None, None, None),
            P(("lat", "ray"), None),
            P(),
            P(None, "lat", None),
            P(("lat", "ray"), None),
            P(None, "lat", None),
            P("lat", None),
            P("lat", None),
            P("lat", None),
            P(),
        ),
        out_specs=(
            P(("lat", "ray"), None),
            P(None, "lat", None),
            P("lat", None),
            P("lat", None),
            P("lat", None),
            P(),
        ),
        check_vma=False,
    )
```

```python
import functools

import jax
import jax.numpy as jnp
from jax import lax
from jax.experimental import pallas as pl
from jax.experimental.pallas import tpu as pltpu
from jax.sharding import PartitionSpec as P

EPS = 1e-06
MESH = pl.DeviceIdType.MESH
F32 = jnp.float32
ROWS = 4
VMEM_BYTES = 16 * 1024 * 1024
GROUP = 32


def select(place, values):
    place = place.astype(jnp.bfloat16)
    total, rest = None, values
    for _ in range(3):
        part = rest.astype(jnp.bfloat16)
        rest = rest - part.astype(F32)
        term = jnp.dot(place, part, preferred_element_type=F32)
        total = term if total is None else total + term
    return total


def plane_size(n_lat):
    return 4 if n_lat % 4 == 0 else 1


def partner(at, step, count):
    if count & (count - 1):
        return lax.rem(at + step, count)
    result, bit = 0, 1
    while bit < count:
        result = result + bit * lax.rem(lax.div(at, bit) + step // bit, 2)
        bit *= 2
    return result


def source(at, step, count):
    return partner(at, count - step if count & (count - 1) else step, count)


def each(count, body):
    if count <= 64:
        for step in range(count - 1, 0, -1):
            body(step)
    else:
        lax.fori_loop(1, count, lambda step, carry: (body(count - step), carry)[1], 0)


def deliver(*refs):
    half = (len(refs) - 1) // 2
    sems = refs[-1]
    copies = [
        pltpu.make_async_copy(refs[at], refs[half + at], sems.at[at]) for at in range(half)
    ]
    for copy in copies:
        copy.start()
    for copy in copies:
        copy.wait()


def kernel(
    n_lat,
    n_ray,
    pattern_in,
    offsets_in,
    recurrence_in,
    kernels_in,
    smooth_weight_in,
    u_data_in,
    u_smooth_in,
    right_vector_in,
    direction_in,
    model_estimate_in,
    u_data_new,
    u_smooth_new,
    v_new,
    w_new,
    x_new,
    scalars,
    pattern,
    offsets,
    recurrence,
    held,
    smooth_weight,
    u_data,
    u_smooth,
    direction,
    model_estimate,
    full,
    window,
    padded,
    smooth_raw,
    data_raw,
    contrib,
    message,
    inbox,
    square,
    squares,
    local_sem,
    band_sem,
    send_sem,
    recv_sem,
):
    lat = lax.axis_index("lat")
    ray = lax.axis_index("ray")
    n_dev = n_lat * n_ray
    me = lat * n_ray + ray
    blocks_dev, kernel_count, block, _ = held.shape
    tiles_dev = right_vector_in.shape[0]
    stencil = smooth_weight.shape[0]
    slots = blocks_dev * kernel_count
    cell_count = n_lat * tiles_dev * block
    rows_all = n_dev * blocks_dev * block + stencil * cell_count
    ratio = cell_count / rows_all

    n_inner = plane_size(n_lat)
    n_outer = n_lat // n_inner
    outer, inner = lax.div(lat, n_inner), lax.rem(lat, n_inner)

    barrier = pltpu.get_barrier_semaphore()

    def greet(device):
        pl.semaphore_signal(barrier, inc=1, device_id=device, device_id_type=MESH)

    def greet_all(step):
        greet((partner(lat, step // n_ray, n_lat), partner(ray, step % n_ray, n_ray)))

    each(n_dev, greet_all)

    def band_of(index):
        return full.at[pl.ds(pl.multiple_of(index * tiles_dev, tiles_dev), tiles_dev)]

    own_band = pltpu.make_async_copy(right_vector_in, band_of(lat), local_sem.at[0])
    own_band.start()
    fetches = [
        pltpu.make_async_copy(source, target, local_sem.at[1 + at])
        for at, (source, target) in enumerate(
            (
                (pattern_in, pattern),
                (offsets_in, offsets),
                (recurrence_in, recurrence),
                (smooth_weight_in, smooth_weight),
                (u_data_in, u_data),
                (u_smooth_in, u_smooth),
                (direction_in, direction),
                (model_estimate_in, model_estimate),
                (kernels_in, held),
            )
        )
    ]
    for fetch in fetches:
        fetch.start()
    own_band.wait()
    pl.semaphore_wait(barrier, n_dev - 1)

    def copy_band(index, slot, device):
        return pltpu.make_async_remote_copy(
            src_ref=band_of(index),
            dst_ref=band_of(index),
            send_sem=send_sem.at[0],
            recv_sem=band_sem.at[slot],
            device_id=device,
            device_id_type=MESH,
        )

    def forward(index, slot):
        for step in range(n_inner - 1, 0, -1):
            copy_band(
                index, slot * n_inner + step, (outer * n_inner + partner(inner, step, n_inner), ray)
            ).start()

    for step in range(n_lat - 1, 0, -1):
        copy_band(lat, step, (partner(lat, step, n_lat), ray)).start()
    for fetch in fetches[:3]:
        fetch.wait()

    alpha_old = recurrence[0]
    lane_slot = lax.broadcasted_iota(jnp.int32, (1, slots), 1)
    tile_row = jnp.zeros((1, slots), F32)
    for b in range(blocks_dev):
        for k in range(kernel_count):
            tile_row = jnp.where(
                lane_slot == b * kernel_count + k, pattern[k, b].astype(F32), tile_row
            )
    shape = (n_lat * ROWS, slots)
    message_row = lax.broadcasted_iota(jnp.int32, shape, 0)
    slot = lax.broadcasted_iota(jnp.int32, shape, 1).astype(F32)
    kind = message_row & (ROWS - 1)
    local_tile = tile_row - ((message_row // ROWS) * tiles_dev).astype(F32)
    in_band = (local_tile >= 0) & (local_tile < tiles_dev)
    first = jnp.min(jnp.where(in_band, slot, F32(slots)), axis=1, keepdims=True)
    is_first = in_band & (slot == first)
    is_second = in_band & (slot != first)
    selector = jnp.where(
        (is_first & (kind == 0)) | (is_second & (kind == 1)), F32(1), F32(0)
    )
    first_tile = jnp.sum(jnp.where(is_first, local_tile + 1, F32(0)), axis=1, keepdims=True)
    second_tile = jnp.sum(jnp.where(is_second, local_tile + 1, F32(0)), axis=1, keepdims=True)
    wide = (n_lat * ROWS, block)
    lane_wide = lax.broadcasted_iota(jnp.int32, wide, 1)
    kind_wide = lax.broadcasted_iota(jnp.int32, wide, 0) & (ROWS - 1)
    mark = lax.rem(me, GROUP) * ROWS
    header = jnp.where(
        lane_wide == mark,
        first_tile,
        jnp.where(lane_wide == mark + 1, second_tile, F32(0)),
    )
    header = jnp.where(kind_wide == 2, header, F32(0))
    is_total = (kind_wide == 2) & (lane_wide == mark + 2)

    for fetch in fetches[3:]:
        fetch.wait()
    for step in range(1, n_lat):
        copy_band(lat, step, (lat, ray)).wait_recv()

    diagonal = lax.broadcasted_iota(jnp.int32, (block, block), 0) == lax.broadcasted_iota(
        jnp.int32, (block, block), 1
    )
    for b in range(blocks_dev):
        total = jnp.where(diagonal, -alpha_old * u_data[b : b + 1, :], F32(0))
        for k in range(kernel_count):
            total = total + held[b, k] * full[pl.ds(pattern[k, b], 1), :]
        column = jnp.sum(total, axis=1, keepdims=True)
        data_raw[b : b + 1, :] = jnp.sum(
            jnp.where(diagonal, column, F32(0)), axis=0, keepdims=True
        )
        for k in range(kernel_count):
            contrib[b * kernel_count + k : b * kernel_count + k + 1, :] = jnp.sum(
                held[b, k] * column, axis=0, keepdims=True
            )

    own = full[pl.ds(pl.multiple_of(lat * tiles_dev, tiles_dev), tiles_dev), :]
    lane = lax.broadcasted_iota(jnp.int32, (1, block), 1)
    window[0:tiles_dev, :] = own
    window[tiles_dev : tiles_dev + 1, :] = full[
        pl.ds(lax.rem(lat + 1, n_lat) * tiles_dev, 1), :
    ]
    below = window[1 : tiles_dev + 1, :]
    rim = jnp.zeros((1, block), F32)
    smooth_square = jnp.zeros((tiles_dev, block), F32)
    for s in range(stencil):
        offset = offsets[s]
        back = (block - offset) & (block - 1)
        ahead = jnp.where(
            lane < block - offset, pltpu.roll(own, back, 1), pltpu.roll(below, back, 1)
        )
        raw = smooth_weight[s] * (own - ahead) - alpha_old * u_smooth[s]
        smooth_raw[s] = raw
        smooth_square = smooth_square + raw * raw
        weighted = smooth_weight[s] * raw
        padded[s, 8 : 8 + tiles_dev, :] = weighted
        turned = pltpu.roll(weighted, offset & (block - 1), 1)
        rim = rim + jnp.where(lane < offset, turned[tiles_dev - 1 : tiles_dev, :], F32(0))
    raw = data_raw[...]
    row_sum = jnp.sum(raw * raw, axis=0, keepdims=True) + (
        jnp.sum(smooth_square, axis=0, keepdims=True) * (1.0 / n_ray)
    )
    local_total = jnp.sum(row_sum, axis=1, keepdims=True)

    picked = select(selector, contrib[...])
    outgoing = (
        picked
        + header
        + jnp.where(is_total, local_total, F32(0))
        + jnp.where(kind_wide == 3, rim, F32(0))
    )
    for band in range(n_lat):
        message[band] = outgoing[band * ROWS : (band + 1) * ROWS, :]

    def send_message(step):
        row = partner(lat, step // n_ray, n_lat)
        core = partner(ray, step % n_ray, n_ray)
        pltpu.make_async_remote_copy(
            src_ref=message.at[row],
            dst_ref=inbox.at[me],
            send_sem=send_sem.at[1],
            recv_sem=recv_sem.at[0],
            device_id=(row, core),
            device_id_type=MESH,
        ).start()

    each(n_dev, send_message)
    inbox[me] = message[lat]

    smooth_adjoint = jnp.zeros((tiles_dev, block), F32)
    for s in range(stencil):
        offset = offsets[s]
        padded[s, 7:8, :] = jnp.zeros((1, block), F32)
        weighted = padded[s, 8 : 8 + tiles_dev, :]
        above = padded[s, 7 : 7 + tiles_dev, :]
        behind = jnp.where(
            lane >= offset,
            pltpu.roll(weighted, offset & (block - 1), 1),
            pltpu.roll(above, offset & (block - 1), 1),
        )
        smooth_adjoint = smooth_adjoint + (weighted - behind)

    for _ in range(n_lat - 1):
        copy_band(lat, 0, (lat, ray)).wait_send()
    others = pl.ds(0, n_dev - 1)
    messages = pltpu.make_async_remote_copy(
        src_ref=inbox.at[others],
        dst_ref=inbox.at[others],
        send_sem=send_sem.at[1],
        recv_sem=recv_sem.at[0],
        device_id=(lat, ray),
        device_id_type=MESH,
    )
    messages.wait_recv()

    group = min(GROUP, n_dev)
    lane_group = lax.broadcasted_iota(jnp.int32, (1, group * ROWS), 1)
    tile_group = lax.broadcasted_iota(jnp.int32, (tiles_dev, group * ROWS), 0)
    lane_kind = lane_group & (ROWS - 1)
    west = lax.rem(lat + n_lat - 1, n_lat) * n_ray
    adjoint = smooth_adjoint
    row_total = jnp.zeros((1, 1), F32)
    for start in range(0, n_dev, group):
        letters = inbox[start : start + group]
        heads = jnp.sum(letters[:, 2, :], axis=0, keepdims=True)[:, : group * ROWS]
        row_total = row_total + jnp.sum(
            jnp.where(lane_kind == 2, heads, F32(0)), axis=1, keepdims=True
        )
        place = jnp.where(
            (lane_kind < 2) & (heads == (tile_group + 1).astype(F32)), F32(1), F32(0)
        )
        place = jnp.where(
            (tile_group == 0) & (lane_group == (west - start) * ROWS + 3), F32(-1), place
        )
        adjoint = adjoint + select(place, letters.reshape(group * ROWS, block))

    beta = jnp.sqrt(row_total / rows_all + EPS)
    v_raw = adjoint * (ratio / beta) - beta * own
    square_row = jnp.sum(v_raw * v_raw, axis=0, keepdims=True)
    square[...] = square_row
    squares[lat] = square_row

    def send_square(step):
        pltpu.make_async_remote_copy(
            src_ref=square,
            dst_ref=squares.at[lat],
            send_sem=send_sem.at[2],
            recv_sem=recv_sem.at[1],
            device_id=(partner(lat, step, n_lat), ray),
            device_id_type=MESH,
        ).start()

    each(n_lat, send_square)

    rhobar_old = recurrence[1]
    phibar_old = recurrence[2]
    rho = jnp.sqrt(rhobar_old * rhobar_old + beta * beta)
    cosine = rhobar_old / rho
    sine = beta / rho
    phi = cosine * phibar_old
    phibar = sine * phibar_old
    u_data_new[...] = data_raw[...] / beta
    for s in range(stencil):
        u_smooth_new[s] = smooth_raw[s] / beta
    x_new[...] = model_estimate[...] + phi / rho * direction[...]
    scalars[1] = beta[0, 0]
    scalars[3] = phibar[0, 0]
    messages.wait_send()

    peers = pl.ds(0, n_lat - 1)
    sums = pltpu.make_async_remote_copy(
        src_ref=squares.at[peers],
        dst_ref=squares.at[peers],
        send_sem=send_sem.at[2],
        recv_sem=recv_sem.at[1],
        device_id=(lat, ray),
        device_id_type=MESH,
    )
    sums.wait_recv()
    model_square = jnp.sum(jnp.sum(squares[...], axis=0), axis=1, keepdims=True)
    alpha = jnp.sqrt(model_square / cell_count + EPS)
    theta = sine * alpha
    new = v_raw / alpha
    v_new[...] = new
    w_new[...] = new - theta / rho * direction[...]
    scalars[0] = alpha[0, 0]
    scalars[2] = (-cosine * alpha)[0, 0]
    sums.wait_send()


def local(
    kernels,
    pattern,
    offsets,
    smooth_weight,
    u_data,
    u_smooth,
    right_vector,
    direction,
    model_estimate,
    recurrence,
):
    n_lat = lax.axis_size("lat")
    n_ray = lax.axis_size("ray")
    n_dev = n_lat * n_ray
    blocks_dev, kernel_count, block, _ = kernels.shape
    tiles_dev = right_vector.shape[0]
    stencil = offsets.shape[0]
    smem = pl.BlockSpec(memory_space=pltpu.SMEM)
    vmem = pl.BlockSpec(memory_space=pltpu.VMEM)
    like = lambda x: jax.ShapeDtypeStruct(x.shape, F32)
    n_inner = plane_size(n_lat)
    results = pl.pallas_call(
        functools.partial(kernel, n_lat, n_ray),
        out_shape=(
            like(u_data),
            like(u_smooth),
            like(right_vector),
            like(right_vector),
            like(right_vector),
            jax.ShapeDtypeStruct((4,), F32),
        ),
        in_specs=[pl.BlockSpec(memory_space=pltpu.HBM)] * 10,
        out_specs=(vmem, vmem, vmem, vmem, vmem, smem),
        scratch_shapes=[
            pltpu.SMEM((kernel_count, blocks_dev), jnp.int32),
            pltpu.SMEM(offsets.shape, jnp.int32),
            pltpu.SMEM(recurrence.shape, F32),
            pltpu.VMEM(kernels.shape, F32),
            pltpu.VMEM(smooth_weight.shape, F32),
            pltpu.VMEM(u_data.shape, F32),
            pltpu.VMEM(u_smooth.shape, F32),
            pltpu.VMEM(direction.shape, F32),
            pltpu.VMEM(model_estimate.shape, F32),
            pltpu.VMEM((n_lat * tiles_dev, block), F32),
            pltpu.VMEM((tiles_dev + 8, block), F32),
            pltpu.VMEM((stencil, tiles_dev + 8, block), F32),
            pltpu.VMEM((stencil, tiles_dev, block), F32),
            pltpu.VMEM((blocks_dev, block), F32),
            pltpu.VMEM((blocks_dev * kernel_count, block), F32),
            pltpu.VMEM((n_lat, ROWS, block), F32),
            pltpu.VMEM((n_dev, ROWS, block), F32),
            pltpu.VMEM((1, block), F32),
            pltpu.VMEM((n_lat, 1, block), F32),
            pltpu.SemaphoreType.DMA((10,)),
            pltpu.SemaphoreType.DMA((n_lat,)),
            pltpu.SemaphoreType.DMA((3,)),
            pltpu.SemaphoreType.DMA((2,)),
        ],
        compiler_params=pltpu.CompilerParams(
            collective_id=0, has_side_effects=True, vmem_limit_bytes=VMEM_BYTES
        ),
    )(
        *(
            pltpu.with_memory_space_constraint(x, pltpu.HBM)
            for x in (
                pattern.T,
                offsets,
                recurrence,
                kernels,
                smooth_weight,
                u_data,
                u_smooth,
                right_vector,
                direction,
                model_estimate,
            )
        )
    )
    return pl.pallas_call(
        deliver,
        out_shape=tuple(like(x) for x in results),
        in_specs=[vmem] * 5 + [smem],
        out_specs=(pl.BlockSpec(memory_space=pltpu.HBM),) * 6,
        scratch_shapes=[pltpu.SemaphoreType.DMA((6,))],
        compiler_params=pltpu.CompilerParams(vmem_limit_bytes=VMEM_BYTES),
    )(*results)


def solution(mesh):
    return jax.shard_map(
        local,
        mesh=mesh,
        in_specs=(
            P(("lat", "ray"), None, None, None),
            P(("lat", "ray"), None),
            P(),
            P(None, "lat", None),
            P(("lat", "ray"), None),
            P(None, "lat", None),
            P("lat", None),
            P("lat", None),
            P("lat", None),
            P(),
        ),
        out_specs=(
            P(("lat", "ray"), None),
            P(None, "lat", None),
            P("lat", None),
            P("lat", None),
            P("lat", None),
            P(),
        ),
        check_vma=False,
    )
```

```python
import functools

import jax
import jax.numpy as jnp
from jax import lax
from jax.experimental import pallas as pl
from jax.experimental.pallas import tpu as pltpu
from jax.sharding import PartitionSpec as P

EPS = 1e-06
MESH = pl.DeviceIdType.MESH
F32 = jnp.float32
ROWS = 4
VMEM_BYTES = 16 * 1024 * 1024
GROUP = 32


def select(place, values):
    place = place.astype(jnp.bfloat16)
    total, rest = None, values
    for _ in range(3):
        part = rest.astype(jnp.bfloat16)
        rest = rest - part.astype(F32)
        term = jnp.dot(place, part, preferred_element_type=F32)
        total = term if total is None else total + term
    return total


def plane_size(n_lat):
    return 4 if n_lat % 4 == 0 else 1


def partner(at, step, count):
    if count & (count - 1):
        return lax.rem(at + step, count)
    result, bit = 0, 1
    while bit < count:
        result = result + bit * lax.rem(lax.div(at, bit) + step // bit, 2)
        bit *= 2
    return result


def source(at, step, count):
    return partner(at, count - step if count & (count - 1) else step, count)


def each(count, body):
    if count <= 64:
        for step in range(count - 1, 0, -1):
            body(step)
    else:
        lax.fori_loop(1, count, lambda step, carry: (body(count - step), carry)[1], 0)


def deliver(*refs):
    half = (len(refs) - 1) // 2
    sems = refs[-1]
    copies = [
        pltpu.make_async_copy(refs[at], refs[half + at], sems.at[at]) for at in range(half)
    ]
    for copy in copies:
        copy.start()
    for copy in copies:
        copy.wait()


def kernel(
    n_lat,
    n_ray,
    pattern_in,
    offsets_in,
    recurrence_in,
    kernels_in,
    smooth_weight_in,
    u_data_in,
    u_smooth_in,
    right_vector_in,
    direction_in,
    model_estimate_in,
    u_data_new,
    u_smooth_new,
    v_new,
    w_new,
    x_new,
    scalars,
    pattern,
    offsets,
    recurrence,
    held,
    smooth_weight,
    u_data,
    u_smooth,
    direction,
    model_estimate,
    full,
    window,
    padded,
    smooth_raw,
    data_raw,
    contrib,
    message,
    inbox,
    square,
    squares,
    local_sem,
    band_sem,
    send_sem,
    recv_sem,
):
    lat = lax.axis_index("lat")
    ray = lax.axis_index("ray")
    n_dev = n_lat * n_ray
    me = lat * n_ray + ray
    blocks_dev, kernel_count, block, _ = held.shape
    tiles_dev = right_vector_in.shape[0]
    stencil = smooth_weight.shape[0]
    slots = blocks_dev * kernel_count
    cell_count = n_lat * tiles_dev * block
    rows_all = n_dev * blocks_dev * block + stencil * cell_count
    ratio = cell_count / rows_all

    n_inner = plane_size(n_lat)
    n_outer = n_lat // n_inner
    outer, inner = lax.div(lat, n_inner), lax.rem(lat, n_inner)

    barrier = pltpu.get_barrier_semaphore()

    def greet(device):
        pl.semaphore_signal(barrier, inc=1, device_id=device, device_id_type=MESH)

    def greet_all(step):
        greet((partner(lat, step // n_ray, n_lat), partner(ray, step % n_ray, n_ray)))

    each(n_dev, greet_all)

    def band_of(index):
        return full.at[pl.ds(pl.multiple_of(index * tiles_dev, tiles_dev), tiles_dev)]

    own_band = pltpu.make_async_copy(right_vector_in, band_of(lat), local_sem.at[0])
    own_band.start()
    fetches = [
        pltpu.make_async_copy(source, target, local_sem.at[1 + at])
        for at, (source, target) in enumerate(
            (
                (pattern_in, pattern),
                (offsets_in, offsets),
                (recurrence_in, recurrence),
                (smooth_weight_in, smooth_weight),
                (u_data_in, u_data),
                (u_smooth_in, u_smooth),
                (direction_in, direction),
                (model_estimate_in, model_estimate),
                (kernels_in, held),
            )
        )
    ]
    for fetch in fetches:
        fetch.start()
    own_band.wait()
    pl.semaphore_wait(barrier, n_dev - 1)

    parts = n_ray if n_ray == 2 and tiles_dev % (8 * n_ray) == 0 else 1
    part_rows = tiles_dev // parts
    part = ray if parts > 1 else 0
    other_ray = partner(ray, 1, n_ray)

    def copy_band(index, which, slot, device):
        rows = pl.ds(
            pl.multiple_of(index * tiles_dev + which * part_rows, part_rows), part_rows
        )
        return pltpu.make_async_remote_copy(
            src_ref=full.at[rows],
            dst_ref=full.at[rows],
            send_sem=send_sem.at[0],
            recv_sem=band_sem.at[slot],
            device_id=device,
            device_id_type=MESH,
        )

    for step in range(n_lat - 1, 0, -1):
        copy_band(lat, part, step, (partner(lat, step, n_lat), ray)).start()
    for fetch in fetches[:3]:
        fetch.wait()

    alpha_old = recurrence[0]
    lane_slot = lax.broadcasted_iota(jnp.int32, (1, slots), 1)
    tile_row = jnp.zeros((1, slots), F32)
    for b in range(blocks_dev):
        for k in range(kernel_count):
            tile_row = jnp.where(
                lane_slot == b * kernel_count + k, pattern[k, b].astype(F32), tile_row
            )
    shape = (n_lat * ROWS, slots)
    message_row = lax.broadcasted_iota(jnp.int32, shape, 0)
    slot = lax.broadcasted_iota(jnp.int32, shape, 1).astype(F32)
    kind = message_row & (ROWS - 1)
    local_tile = tile_row - ((message_row // ROWS) * tiles_dev).astype(F32)
    in_band = (local_tile >= 0) & (local_tile < tiles_dev)
    first = jnp.min(jnp.where(in_band, slot, F32(slots)), axis=1, keepdims=True)
    is_first = in_band & (slot == first)
    is_second = in_band & (slot != first)
    selector = jnp.where(
        (is_first & (kind == 0)) | (is_second & (kind == 1)), F32(1), F32(0)
    )
    first_tile = jnp.sum(jnp.where(is_first, local_tile + 1, F32(0)), axis=1, keepdims=True)
    second_tile = jnp.sum(jnp.where(is_second, local_tile + 1, F32(0)), axis=1, keepdims=True)
    wide = (n_lat * ROWS, block)
    lane_wide = lax.broadcasted_iota(jnp.int32, wide, 1)
    kind_wide = lax.broadcasted_iota(jnp.int32, wide, 0) & (ROWS - 1)
    mark = lax.rem(me, GROUP) * ROWS
    header = jnp.where(
        lane_wide == mark,
        first_tile,
        jnp.where(lane_wide == mark + 1, second_tile, F32(0)),
    )
    header = jnp.where(kind_wide == 2, header, F32(0))
    is_total = (kind_wide == 2) & (lane_wide == mark + 2)

    for step in range(1, n_lat):
        index = source(lat, step, n_lat)
        copy_band(index, part, step, (lat, ray)).wait_recv()
        if parts > 1:
            copy_band(index, part, n_lat + step, (lat, other_ray)).start()
    for fetch in fetches[3:]:
        fetch.wait()
    if parts > 1:
        for step in range(1, n_lat):
            copy_band(
                source(lat, step, n_lat), other_ray, n_lat + step, (lat, ray)
            ).wait_recv()

    diagonal = lax.broadcasted_iota(jnp.int32, (block, block), 0) == lax.broadcasted_iota(
        jnp.int32, (block, block), 1
    )
    for b in range(blocks_dev):
        total = jnp.where(diagonal, -alpha_old * u_data[b : b + 1, :], F32(0))
        for k in range(kernel_count):
            total = total + held[b, k] * full[pl.ds(pattern[k, b], 1), :]
        column = jnp.sum(total, axis=1, keepdims=True)
        data_raw[b : b + 1, :] = jnp.sum(
            jnp.where(diagonal, column, F32(0)), axis=0, keepdims=True
        )
        for k in range(kernel_count):
            contrib[b * kernel_count + k : b * kernel_count + k + 1, :] = jnp.sum(
                held[b, k] * column, axis=0, keepdims=True
            )

    own = full[pl.ds(pl.multiple_of(lat * tiles_dev, tiles_dev), tiles_dev), :]
    lane = lax.broadcasted_iota(jnp.int32, (1, block), 1)
    window[0:tiles_dev, :] = own
    window[tiles_dev : tiles_dev + 1, :] = full[
        pl.ds(lax.rem(lat + 1, n_lat) * tiles_dev, 1), :
    ]
    below = window[1 : tiles_dev + 1, :]
    rim = jnp.zeros((1, block), F32)
    smooth_square = jnp.zeros((tiles_dev, block), F32)
    for s in range(stencil):
        offset = offsets[s]
        back = (block - offset) & (block - 1)
        ahead = jnp.where(
            lane < block - offset, pltpu.roll(own, back, 1), pltpu.roll(below, back, 1)
        )
        raw = smooth_weight[s] * (own - ahead) - alpha_old * u_smooth[s]
        smooth_raw[s] = raw
        smooth_square = smooth_square + raw * raw
        weighted = smooth_weight[s] * raw
        padded[s, 8 : 8 + tiles_dev, :] = weighted
        turned = pltpu.roll(weighted, offset & (block - 1), 1)
        rim = rim + jnp.where(lane < offset, turned[tiles_dev - 1 : tiles_dev, :], F32(0))
    raw = data_raw[...]
    row_sum = jnp.sum(raw * raw, axis=0, keepdims=True) + (
        jnp.sum(smooth_square, axis=0, keepdims=True) * (1.0 / n_ray)
    )
    local_total = jnp.sum(row_sum, axis=1, keepdims=True)

    picked = select(selector, contrib[...])
    outgoing = (
        picked
        + header
        + jnp.where(is_total, local_total, F32(0))
        + jnp.where(kind_wide == 3, rim, F32(0))
    )
    for band in range(n_lat):
        message[band] = outgoing[band * ROWS : (band + 1) * ROWS, :]

    def send_message(step):
        row = partner(lat, step // n_ray, n_lat)
        core = partner(ray, step % n_ray, n_ray)
        pltpu.make_async_remote_copy(
            src_ref=message.at[row],
            dst_ref=inbox.at[me],
            send_sem=send_sem.at[1],
            recv_sem=recv_sem.at[0],
            device_id=(row, core),
            device_id_type=MESH,
        ).start()

    each(n_dev, send_message)
    inbox[me] = message[lat]

    smooth_adjoint = jnp.zeros((tiles_dev, block), F32)
    for s in range(stencil):
        offset = offsets[s]
        padded[s, 7:8, :] = jnp.zeros((1, block), F32)
        weighted = padded[s, 8 : 8 + tiles_dev, :]
        above = padded[s, 7 : 7 + tiles_dev, :]
        behind = jnp.where(
            lane >= offset,
            pltpu.roll(weighted, offset & (block - 1), 1),
            pltpu.roll(above, offset & (block - 1), 1),
        )
        smooth_adjoint = smooth_adjoint + (weighted - behind)

    for _ in range((n_lat - 1) * parts):
        copy_band(lat, part, 0, (lat, ray)).wait_send()
    others = pl.ds(0, n_dev - 1)
    messages = pltpu.make_async_remote_copy(
        src_ref=inbox.at[others],
        dst_ref=inbox.at[others],
        send_sem=send_sem.at[1],
        recv_sem=recv_sem.at[0],
        device_id=(lat, ray),
        device_id_type=MESH,
    )
    messages.wait_recv()

    group = min(GROUP, n_dev)
    lane_group = lax.broadcasted_iota(jnp.int32, (1, group * ROWS), 1)
    tile_group = lax.broadcasted_iota(jnp.int32, (tiles_dev, group * ROWS), 0)
    lane_kind = lane_group & (ROWS - 1)
    west = lax.rem(lat + n_lat - 1, n_lat) * n_ray
    adjoint = smooth_adjoint
    row_total = jnp.zeros((1, 1), F32)
    for start in range(0, n_dev, group):
        letters = inbox[start : start + group]
        heads = jnp.sum(letters[:, 2, :], axis=0, keepdims=True)[:, : group * ROWS]
        row_total = row_total + jnp.sum(
            jnp.where(lane_kind == 2, heads, F32(0)), axis=1, keepdims=True
        )
        place = jnp.where(
            (lane_kind < 2) & (heads == (tile_group + 1).astype(F32)), F32(1), F32(0)
        )
        place = jnp.where(
            (tile_group == 0) & (lane_group == (west - start) * ROWS + 3), F32(-1), place
        )
        adjoint = adjoint + select(place, letters.reshape(group * ROWS, block))

    beta = jnp.sqrt(row_total / rows_all + EPS)
    v_raw = adjoint * (ratio / beta) - beta * own
    square_row = jnp.sum(v_raw * v_raw, axis=0, keepdims=True)
    square[...] = square_row
    squares[lat] = square_row

    def send_square(step):
        pltpu.make_async_remote_copy(
            src_ref=square,
            dst_ref=squares.at[lat],
            send_sem=send_sem.at[2],
            recv_sem=recv_sem.at[1],
            device_id=(partner(lat, step, n_lat), ray),
            device_id_type=MESH,
        ).start()

    each(n_lat, send_square)

    rhobar_old = recurrence[1]
    phibar_old = recurrence[2]
    rho = jnp.sqrt(rhobar_old * rhobar_old + beta * beta)
    cosine = rhobar_old / rho
    sine = beta / rho
    phi = cosine * phibar_old
    phibar = sine * phibar_old
    u_data_new[...] = data_raw[...] / beta
    for s in range(stencil):
        u_smooth_new[s] = smooth_raw[s] / beta
    x_new[...] = model_estimate[...] + phi / rho * direction[...]
    scalars[1] = beta[0, 0]
    scalars[3] = phibar[0, 0]
    messages.wait_send()

    peers = pl.ds(0, n_lat - 1)
    sums = pltpu.make_async_remote_copy(
        src_ref=squares.at[peers],
        dst_ref=squares.at[peers],
        send_sem=send_sem.at[2],
        recv_sem=recv_sem.at[1],
        device_id=(lat, ray),
        device_id_type=MESH,
    )
    sums.wait_recv()
    model_square = jnp.sum(jnp.sum(squares[...], axis=0), axis=1, keepdims=True)
    alpha = jnp.sqrt(model_square / cell_count + EPS)
    theta = sine * alpha
    new = v_raw / alpha
    v_new[...] = new
    w_new[...] = new - theta / rho * direction[...]
    scalars[0] = alpha[0, 0]
    scalars[2] = (-cosine * alpha)[0, 0]
    sums.wait_send()


def local(
    kernels,
    pattern,
    offsets,
    smooth_weight,
    u_data,
    u_smooth,
    right_vector,
    direction,
    model_estimate,
    recurrence,
):
    n_lat = lax.axis_size("lat")
    n_ray = lax.axis_size("ray")
    n_dev = n_lat * n_ray
    blocks_dev, kernel_count, block, _ = kernels.shape
    tiles_dev = right_vector.shape[0]
    stencil = offsets.shape[0]
    smem = pl.BlockSpec(memory_space=pltpu.SMEM)
    vmem = pl.BlockSpec(memory_space=pltpu.VMEM)
    like = lambda x: jax.ShapeDtypeStruct(x.shape, F32)
    n_inner = plane_size(n_lat)
    results = pl.pallas_call(
        functools.partial(kernel, n_lat, n_ray),
        out_shape=(
            like(u_data),
            like(u_smooth),
            like(right_vector),
            like(right_vector),
            like(right_vector),
            jax.ShapeDtypeStruct((4,), F32),
        ),
        in_specs=[pl.BlockSpec(memory_space=pltpu.HBM)] * 10,
        out_specs=(vmem, vmem, vmem, vmem, vmem, smem),
        scratch_shapes=[
            pltpu.SMEM((kernel_count, blocks_dev), jnp.int32),
            pltpu.SMEM(offsets.shape, jnp.int32),
            pltpu.SMEM(recurrence.shape, F32),
            pltpu.VMEM(kernels.shape, F32),
            pltpu.VMEM(smooth_weight.shape, F32),
            pltpu.VMEM(u_data.shape, F32),
            pltpu.VMEM(u_smooth.shape, F32),
            pltpu.VMEM(direction.shape, F32),
            pltpu.VMEM(model_estimate.shape, F32),
            pltpu.VMEM((n_lat * tiles_dev, block), F32),
            pltpu.VMEM((tiles_dev + 8, block), F32),
            pltpu.VMEM((stencil, tiles_dev + 8, block), F32),
            pltpu.VMEM((stencil, tiles_dev, block), F32),
            pltpu.VMEM((blocks_dev, block), F32),
            pltpu.VMEM((blocks_dev * kernel_count, block), F32),
            pltpu.VMEM((n_lat, ROWS, block), F32),
            pltpu.VMEM((n_dev, ROWS, block), F32),
            pltpu.VMEM((1, block), F32),
            pltpu.VMEM((n_lat, 1, block), F32),
            pltpu.SemaphoreType.DMA((10,)),
            pltpu.SemaphoreType.DMA((2 * n_lat,)),
            pltpu.SemaphoreType.DMA((3,)),
            pltpu.SemaphoreType.DMA((2,)),
        ],
        compiler_params=pltpu.CompilerParams(
            collective_id=0, has_side_effects=True, vmem_limit_bytes=VMEM_BYTES
        ),
    )(
        *(
            pltpu.with_memory_space_constraint(x, pltpu.HBM)
            for x in (
                pattern.T,
                offsets,
                recurrence,
                kernels,
                smooth_weight,
                u_data,
                u_smooth,
                right_vector,
                direction,
                model_estimate,
            )
        )
    )
    return pl.pallas_call(
        deliver,
        out_shape=tuple(like(x) for x in results),
        in_specs=[vmem] * 5 + [smem],
        out_specs=(pl.BlockSpec(memory_space=pltpu.HBM),) * 6,
        scratch_shapes=[pltpu.SemaphoreType.DMA((6,))],
        compiler_params=pltpu.CompilerParams(vmem_limit_bytes=VMEM_BYTES),
    )(*results)


def solution(mesh):
    return jax.shard_map(
        local,
        mesh=mesh,
        in_specs=(
            P(("lat", "ray"), None, None, None),
            P(("lat", "ray"), None),
            P(),
            P(None, "lat", None),
            P(("lat", "ray"), None),
            P(None, "lat", None),
            P("lat", None),
            P("lat", None),
            P("lat", None),
            P(),
        ),
        out_specs=(
            P(("lat", "ray"), None),
            P(None, "lat", None),
            P("lat", None),
            P("lat", None),
            P("lat", None),
            P(),
        ),
        check_vma=False,
    )
```

```python
import functools

import jax
import jax.numpy as jnp
from jax import lax
from jax.experimental import pallas as pl
from jax.experimental.pallas import tpu as pltpu
from jax.sharding import PartitionSpec as P

EPS = 1e-06
MESH = pl.DeviceIdType.MESH
F32 = jnp.float32
ROWS = 4
VMEM_BYTES = 16 * 1024 * 1024
GROUP = 32


def select(place, values):
    place = place.astype(jnp.bfloat16)
    total, rest = None, values
    for _ in range(3):
        part = rest.astype(jnp.bfloat16)
        rest = rest - part.astype(F32)
        term = jnp.dot(place, part, preferred_element_type=F32)
        total = term if total is None else total + term
    return total


def plane_size(n_lat):
    return 4 if n_lat % 4 == 0 else 1


def partner(at, step, count):
    if count & (count - 1):
        return lax.rem(at + step, count)
    result, bit = 0, 1
    while bit < count:
        result = result + bit * lax.rem(lax.div(at, bit) + step // bit, 2)
        bit *= 2
    return result


def source(at, step, count):
    return partner(at, count - step if count & (count - 1) else step, count)


def each(count, body):
    if count <= 64:
        for step in range(count - 1, 0, -1):
            body(step)
    else:
        lax.fori_loop(1, count, lambda step, carry: (body(count - step), carry)[1], 0)


def deliver(*refs):
    half = (len(refs) - 1) // 2
    sems = refs[-1]
    copies = [
        pltpu.make_async_copy(refs[at], refs[half + at], sems.at[at]) for at in range(half)
    ]
    for copy in copies:
        copy.start()
    for copy in copies:
        copy.wait()


def kernel(
    n_lat,
    n_ray,
    pattern_in,
    offsets_in,
    recurrence_in,
    kernels_in,
    smooth_weight_in,
    u_data_in,
    u_smooth_in,
    right_vector_in,
    direction_in,
    model_estimate_in,
    u_data_new,
    u_smooth_new,
    v_new,
    w_new,
    x_new,
    scalars,
    pattern,
    offsets,
    recurrence,
    held,
    smooth_weight,
    u_data,
    u_smooth,
    direction,
    model_estimate,
    full,
    window,
    padded,
    smooth_raw,
    data_raw,
    contrib,
    message,
    inbox,
    square,
    squares,
    local_sem,
    band_sem,
    send_sem,
    recv_sem,
):
    lat = lax.axis_index("lat")
    ray = lax.axis_index("ray")
    n_dev = n_lat * n_ray
    me = lat * n_ray + ray
    blocks_dev, kernel_count, block, _ = held.shape
    tiles_dev = right_vector_in.shape[0]
    stencil = smooth_weight.shape[0]
    slots = blocks_dev * kernel_count
    cell_count = n_lat * tiles_dev * block
    rows_all = n_dev * blocks_dev * block + stencil * cell_count
    ratio = cell_count / rows_all

    n_inner = plane_size(n_lat)
    n_outer = n_lat // n_inner
    outer, inner = lax.div(lat, n_inner), lax.rem(lat, n_inner)

    barrier = pltpu.get_barrier_semaphore()

    def greet(device):
        pl.semaphore_signal(barrier, inc=1, device_id=device, device_id_type=MESH)

    def greet_all(step):
        greet((partner(lat, step // n_ray, n_lat), partner(ray, step % n_ray, n_ray)))

    each(n_dev, greet_all)

    def band_of(index):
        return full.at[pl.ds(pl.multiple_of(index * tiles_dev, tiles_dev), tiles_dev)]

    own_band = pltpu.make_async_copy(right_vector_in, band_of(lat), local_sem.at[0])
    own_band.start()
    fetches = [
        pltpu.make_async_copy(source, target, local_sem.at[1 + at])
        for at, (source, target) in enumerate(
            (
                (pattern_in, pattern),
                (offsets_in, offsets),
                (recurrence_in, recurrence),
                (smooth_weight_in, smooth_weight),
                (u_data_in, u_data),
                (u_smooth_in, u_smooth),
                (direction_in, direction),
                (model_estimate_in, model_estimate),
                (kernels_in, held),
            )
        )
    ]
    for fetch in fetches:
        fetch.start()
    own_band.wait()
    pl.semaphore_wait(barrier, n_dev - 1)

    parts = n_ray if n_ray == 2 and tiles_dev % (8 * n_ray) == 0 else 1
    part_rows = tiles_dev // parts
    part = ray if parts > 1 else 0
    other_ray = partner(ray, 1, n_ray)

    def copy_band(index, which, slot, device):
        rows = pl.ds(
            pl.multiple_of(index * tiles_dev + which * part_rows, part_rows), part_rows
        )
        return pltpu.make_async_remote_copy(
            src_ref=full.at[rows],
            dst_ref=full.at[rows],
            send_sem=send_sem.at[0],
            recv_sem=band_sem.at[slot],
            device_id=device,
            device_id_type=MESH,
        )

    for step in range(n_lat - 1, 0, -1):
        copy_band(lat, part, step, (partner(lat, step, n_lat), ray)).start()
    for fetch in fetches[:3]:
        fetch.wait()

    alpha_old = recurrence[0]
    lane_slot = lax.broadcasted_iota(jnp.int32, (1, slots), 1)
    tile_row = jnp.zeros((1, slots), F32)
    for b in range(blocks_dev):
        for k in range(kernel_count):
            tile_row = jnp.where(
                lane_slot == b * kernel_count + k, pattern[k, b].astype(F32), tile_row
            )
    shape = (n_lat * ROWS, slots)
    message_row = lax.broadcasted_iota(jnp.int32, shape, 0)
    slot = lax.broadcasted_iota(jnp.int32, shape, 1).astype(F32)
    kind = message_row & (ROWS - 1)
    local_tile = tile_row - ((message_row // ROWS) * tiles_dev).astype(F32)
    in_band = (local_tile >= 0) & (local_tile < tiles_dev)
    first = jnp.min(jnp.where(in_band, slot, F32(slots)), axis=1, keepdims=True)
    is_first = in_band & (slot == first)
    is_second = in_band & (slot != first)
    selector = jnp.where(
        (is_first & (kind == 0)) | (is_second & (kind == 1)), F32(1), F32(0)
    )
    first_tile = jnp.sum(jnp.where(is_first, local_tile + 1, F32(0)), axis=1, keepdims=True)
    second_tile = jnp.sum(jnp.where(is_second, local_tile + 1, F32(0)), axis=1, keepdims=True)
    wide = (n_lat * ROWS, block)
    lane_wide = lax.broadcasted_iota(jnp.int32, wide, 1)
    kind_wide = lax.broadcasted_iota(jnp.int32, wide, 0) & (ROWS - 1)
    mark = lax.rem(me, GROUP) * ROWS
    header = jnp.where(
        lane_wide == mark,
        first_tile,
        jnp.where(lane_wide == mark + 1, second_tile, F32(0)),
    )
    header = jnp.where(kind_wide == 2, header, F32(0))
    is_total = (kind_wide == 2) & (lane_wide == mark + 2)

    for step in range(1, n_lat):
        index = source(lat, step, n_lat)
        copy_band(index, part, step, (lat, ray)).wait_recv()
        if parts > 1:
            copy_band(index, part, n_lat + step, (lat, other_ray)).start()
    for fetch in fetches[3:]:
        fetch.wait()
    if parts > 1:
        for step in range(1, n_lat):
            copy_band(
                source(lat, step, n_lat), other_ray, n_lat + step, (lat, ray)
            ).wait_recv()

    diagonal = lax.broadcasted_iota(jnp.int32, (block, block), 0) == lax.broadcasted_iota(
        jnp.int32, (block, block), 1
    )
    for b in range(blocks_dev):
        total = jnp.where(diagonal, -alpha_old * u_data[b : b + 1, :], F32(0))
        for k in range(kernel_count):
            total = total + held[b, k] * full[pl.ds(pattern[k, b], 1), :]
        column = jnp.sum(total, axis=1, keepdims=True)
        data_raw[b : b + 1, :] = jnp.sum(
            jnp.where(diagonal, column, F32(0)), axis=0, keepdims=True
        )
        for k in range(kernel_count):
            contrib[b * kernel_count + k : b * kernel_count + k + 1, :] = jnp.sum(
                held[b, k] * column, axis=0, keepdims=True
            )

    own = full[pl.ds(pl.multiple_of(lat * tiles_dev, tiles_dev), tiles_dev), :]
    lane = lax.broadcasted_iota(jnp.int32, (1, block), 1)
    window[0:tiles_dev, :] = own
    window[tiles_dev : tiles_dev + 1, :] = full[
        pl.ds(lax.rem(lat + 1, n_lat) * tiles_dev, 1), :
    ]
    below = window[1 : tiles_dev + 1, :]
    rim = jnp.zeros((1, block), F32)
    smooth_square = jnp.zeros((tiles_dev, block), F32)
    for s in range(stencil):
        offset = offsets[s]
        back = (block - offset) & (block - 1)
        ahead = jnp.where(
            lane < block - offset, pltpu.roll(own, back, 1), pltpu.roll(below, back, 1)
        )
        raw = smooth_weight[s] * (own - ahead) - alpha_old * u_smooth[s]
        smooth_raw[s] = raw
        smooth_square = smooth_square + raw * raw
        weighted = smooth_weight[s] * raw
        padded[s, 8 : 8 + tiles_dev, :] = weighted
        turned = pltpu.roll(weighted, offset & (block - 1), 1)
        rim = rim + jnp.where(lane < offset, turned[tiles_dev - 1 : tiles_dev, :], F32(0))
    raw = data_raw[...]
    row_sum = jnp.sum(raw * raw, axis=0, keepdims=True) + (
        jnp.sum(smooth_square, axis=0, keepdims=True) * (1.0 / n_ray)
    )
    local_total = jnp.sum(row_sum, axis=1, keepdims=True)

    picked = select(selector, contrib[...])
    outgoing = (
        picked
        + header
        + jnp.where(is_total, local_total, F32(0))
        + jnp.where(kind_wide == 3, rim, F32(0))
    )
    for band in range(n_lat):
        message[band] = outgoing[band * ROWS : (band + 1) * ROWS, :]

    def send_message(step):
        row = partner(lat, step // n_ray, n_lat)
        core = partner(ray, step % n_ray, n_ray)
        pltpu.make_async_remote_copy(
            src_ref=message.at[row],
            dst_ref=inbox.at[me],
            send_sem=send_sem.at[1],
            recv_sem=recv_sem.at[0],
            device_id=(row, core),
            device_id_type=MESH,
        ).start()

    each(n_dev, send_message)
    inbox[me] = message[lat]

    smooth_adjoint = jnp.zeros((tiles_dev, block), F32)
    for s in range(stencil):
        offset = offsets[s]
        padded[s, 7:8, :] = jnp.zeros((1, block), F32)
        weighted = padded[s, 8 : 8 + tiles_dev, :]
        above = padded[s, 7 : 7 + tiles_dev, :]
        behind = jnp.where(
            lane >= offset,
            pltpu.roll(weighted, offset & (block - 1), 1),
            pltpu.roll(above, offset & (block - 1), 1),
        )
        smooth_adjoint = smooth_adjoint + (weighted - behind)

    for _ in range((n_lat - 1) * parts):
        copy_band(lat, part, 0, (lat, ray)).wait_send()
    others = pl.ds(0, n_dev - 1)
    messages = pltpu.make_async_remote_copy(
        src_ref=inbox.at[others],
        dst_ref=inbox.at[others],
        send_sem=send_sem.at[1],
        recv_sem=recv_sem.at[0],
        device_id=(lat, ray),
        device_id_type=MESH,
    )
    messages.wait_recv()

    group = min(GROUP, n_dev)
    lane_group = lax.broadcasted_iota(jnp.int32, (1, group * ROWS), 1)
    tile_group = lax.broadcasted_iota(jnp.int32, (tiles_dev, group * ROWS), 0)
    lane_kind = lane_group & (ROWS - 1)
    west = lax.rem(lat + n_lat - 1, n_lat) * n_ray
    adjoint = smooth_adjoint
    row_total = jnp.zeros((1, 1), F32)
    for start in range(0, n_dev, group):
        letters = inbox[start : start + group]
        heads = jnp.sum(letters[:, 2, :], axis=0, keepdims=True)[:, : group * ROWS]
        row_total = row_total + jnp.sum(
            jnp.where(lane_kind == 2, heads, F32(0)), axis=1, keepdims=True
        )
        place = jnp.where(
            (lane_kind < 2) & (heads == (tile_group + 1).astype(F32)), F32(1), F32(0)
        )
        place = jnp.where(
            (tile_group == 0) & (lane_group == (west - start) * ROWS + 3), F32(-1), place
        )
        adjoint = adjoint + select(place, letters.reshape(group * ROWS, block))

    beta = jnp.sqrt(row_total / rows_all + EPS)
    v_raw = adjoint * (ratio / beta) - beta * own
    square_row = jnp.sum(v_raw * v_raw, axis=0, keepdims=True)
    square[...] = square_row
    squares[pl.ds(lat, 1), :] = square_row

    def send_square(step):
        pltpu.make_async_remote_copy(
            src_ref=square,
            dst_ref=squares.at[pl.ds(lat, 1)],
            send_sem=send_sem.at[2],
            recv_sem=recv_sem.at[1],
            device_id=(partner(lat, step, n_lat), ray),
            device_id_type=MESH,
        ).start()

    each(n_lat, send_square)

    rhobar_old = recurrence[1]
    phibar_old = recurrence[2]
    rho = jnp.sqrt(rhobar_old * rhobar_old + beta * beta)
    cosine = rhobar_old / rho
    sine = beta / rho
    phi = cosine * phibar_old
    phibar = sine * phibar_old
    u_data_new[...] = data_raw[...] / beta
    for s in range(stencil):
        u_smooth_new[s] = smooth_raw[s] / beta
    x_new[...] = model_estimate[...] + phi / rho * direction[...]
    turned_direction = sine / rho * direction[...]
    scalars[1] = beta[0, 0]
    scalars[3] = phibar[0, 0]
    messages.wait_send()

    peers = pl.ds(0, n_lat - 1)
    sums = pltpu.make_async_remote_copy(
        src_ref=squares.at[peers],
        dst_ref=squares.at[peers],
        send_sem=send_sem.at[2],
        recv_sem=recv_sem.at[1],
        device_id=(lat, ray),
        device_id_type=MESH,
    )
    sums.wait_recv()
    model_square = jnp.sum(jnp.sum(squares[...], axis=0, keepdims=True), axis=1, keepdims=True)
    alpha = jnp.sqrt(model_square / cell_count + EPS)
    new = v_raw * (1.0 / alpha)
    v_new[...] = new
    w_new[...] = new - alpha * turned_direction
    scalars[0] = alpha[0, 0]
    scalars[2] = (-cosine * alpha)[0, 0]
    sums.wait_send()


def local(
    kernels,
    pattern,
    offsets,
    smooth_weight,
    u_data,
    u_smooth,
    right_vector,
    direction,
    model_estimate,
    recurrence,
):
    n_lat = lax.axis_size("lat")
    n_ray = lax.axis_size("ray")
    n_dev = n_lat * n_ray
    blocks_dev, kernel_count, block, _ = kernels.shape
    tiles_dev = right_vector.shape[0]
    stencil = offsets.shape[0]
    smem = pl.BlockSpec(memory_space=pltpu.SMEM)
    vmem = pl.BlockSpec(memory_space=pltpu.VMEM)
    like = lambda x: jax.ShapeDtypeStruct(x.shape, F32)
    n_inner = plane_size(n_lat)
    results = pl.pallas_call(
        functools.partial(kernel, n_lat, n_ray),
        out_shape=(
            like(u_data),
            like(u_smooth),
            like(right_vector),
            like(right_vector),
            like(right_vector),
            jax.ShapeDtypeStruct((4,), F32),
        ),
        in_specs=[pl.BlockSpec(memory_space=pltpu.HBM)] * 10,
        out_specs=(vmem, vmem, vmem, vmem, vmem, smem),
        scratch_shapes=[
            pltpu.SMEM((kernel_count, blocks_dev), jnp.int32),
            pltpu.SMEM(offsets.shape, jnp.int32),
            pltpu.SMEM(recurrence.shape, F32),
            pltpu.VMEM(kernels.shape, F32),
            pltpu.VMEM(smooth_weight.shape, F32),
            pltpu.VMEM(u_data.shape, F32),
            pltpu.VMEM(u_smooth.shape, F32),
            pltpu.VMEM(direction.shape, F32),
            pltpu.VMEM(model_estimate.shape, F32),
            pltpu.VMEM((n_lat * tiles_dev, block), F32),
            pltpu.VMEM((tiles_dev + 8, block), F32),
            pltpu.VMEM((stencil, tiles_dev + 8, block), F32),
            pltpu.VMEM((stencil, tiles_dev, block), F32),
            pltpu.VMEM((blocks_dev, block), F32),
            pltpu.VMEM((blocks_dev * kernel_count, block), F32),
            pltpu.VMEM((n_lat, ROWS, block), F32),
            pltpu.VMEM((n_dev, ROWS, block), F32),
            pltpu.VMEM((1, block), F32),
            pltpu.VMEM((n_lat, block), F32),
            pltpu.SemaphoreType.DMA((10,)),
            pltpu.SemaphoreType.DMA((2 * n_lat,)),
            pltpu.SemaphoreType.DMA((3,)),
            pltpu.SemaphoreType.DMA((2,)),
        ],
        compiler_params=pltpu.CompilerParams(
            collective_id=0, has_side_effects=True, vmem_limit_bytes=VMEM_BYTES
        ),
    )(
        *(
            pltpu.with_memory_space_constraint(x, pltpu.HBM)
            for x in (
                pattern.T,
                offsets,
                recurrence,
                kernels,
                smooth_weight,
                u_data,
                u_smooth,
                right_vector,
                direction,
                model_estimate,
            )
        )
    )
    return pl.pallas_call(
        deliver,
        out_shape=tuple(like(x) for x in results),
        in_specs=[vmem] * 5 + [smem],
        out_specs=(pl.BlockSpec(memory_space=pltpu.HBM),) * 6,
        scratch_shapes=[pltpu.SemaphoreType.DMA((6,))],
        compiler_params=pltpu.CompilerParams(vmem_limit_bytes=VMEM_BYTES),
    )(*results)


def solution(mesh):
    return jax.shard_map(
        local,
        mesh=mesh,
        in_specs=(
            P(("lat", "ray"), None, None, None),
            P(("lat", "ray"), None),
            P(),
            P(None, "lat", None),
            P(("lat", "ray"), None),
            P(None, "lat", None),
            P("lat", None),
            P("lat", None),
            P("lat", None),
            P(),
        ),
        out_specs=(
            P(("lat", "ray"), None),
            P(None, "lat", None),
            P("lat", None),
            P("lat", None),
            P("lat", None),
            P(),
        ),
        check_vma=False,
    )
```
